32 devices in a mesh: groups: 2 (over x), tier: 16 (over z, y, core).
Axes of the slice: x: 2, y: 2, z: 4, core: 2. Of those that a mesh axis runs over, the one named last changes fastest.
Arguments:
- rho: float32 [256, 2, 256, 256], P(('groups', 'tier')), parts along dimension 0, may hold values from -6 to 6
- hamiltonian: float32 [256, 256], replicated, may hold values from -0.375 to 0.375
- couplings: float32 [4, 256, 256], replicated, may hold values from -0.375 to 0.375
- bath_coef: float32 [8, 2], P('groups'), parts along dimension 0, may hold values from 0.3 to 1.5
- damping: float32 [256], P(('groups', 'tier')), parts along dimension 0, may hold values from 0.2 to 3
- match_edges: int32 [16, 4, 1, 5], P('tier'), may hold values from 0 to 7, as said below
- left_rows: int32 [16, 6, 5], replicated, may hold values from 0 to 127, as said below
- left_count: int32 [16], replicated, may hold values from 1 to 6, as said below
Outputs:
- rho_next: float32 [256, 2, 256, 256], P(('groups', 'tier')), parts along dimension 0
The draws below stay inside these ranges and needn't reach their ends.
There are 2 independent parts, one for each index of `groups`. The reference program is written for one: setup_inputs(seed, part) draws one part's arguments, and reference() takes and returns one part's arrays. A program takes and returns all parts, laid end to end along the dimension named above; an argument that names none is the same for every part. Nothing has to cross between parts.
Inputs may be any that keep to these rules, and one draw needn't show every extreme that they name: match_edges[b, c, j] = (target slot, partner slot, mode, lower flag 0 or 1, occupation 1 to 3); the row (b XOR 2^c, c, j) describes the same edge from the partner's side: its target slot is this row's partner slot and the reverse, same mode and occupation, opposite lower flag. left_rows[b, j] = (target slot, source matrix index, mode, lower flag 0 or 1, occupation 1 to 3); the source's block lies at cyclic block distance 1 to 4 from b, and the rows of one block name distinct source blocks. Only the first left_count[b] rows of block b are live; some block has exactly 6.
All inputs are finite; a program needn't handle non-finite values.
Results may differ from the reference program's by a relative error of at most 0.00005.
Values sent between devices are 32-bit elements; how exact they have to be, the bound alone decides.
A program may use at most 128 MiB of HBM per device.

```python
import math
import jax
import jax.numpy as jnp
from jax import lax

ORDER = 256
KMODES = 4
COLOURS = 4
PAIRS = 1
LEFT_CAP = 6
REACH = 4
MAT_DEV = 8
MATRICES = 128
N_TIER = 16


def match_tables(key):
    subkeys = jax.random.split(key, 4)
    blocks = jnp.arange(N_TIER, dtype=jnp.int32)
    slot_draw = jax.random.randint(subkeys[0], (COLOURS, N_TIER, PAIRS), 0, MAT_DEV)
    flag_draw = jax.random.randint(subkeys[1], (COLOURS, N_TIER, PAIRS), 0, 2)
    mode_draw = jax.random.randint(subkeys[2], (COLOURS, N_TIER, PAIRS), 0, KMODES)
    occ_draw = jax.random.randint(subkeys[3], (COLOURS, N_TIER, PAIRS), 1, 4)
    colour_rows = []
    for colour in range(COLOURS):
        stride = 2 ** colour
        upper_half = blocks // stride % 2
        partner = blocks + stride - 2 * stride * upper_half
        lowest = jnp.minimum(blocks, partner)
        own_slot = slot_draw[colour]
        their_slot = slot_draw[colour][partner]
        base_flag = flag_draw[colour][lowest]
        lower_flag = jnp.where(upper_half[:, None] == 0, base_flag, 1 - base_flag)
        mode_ids = mode_draw[colour][lowest]
        occupied = occ_draw[colour][lowest]
        colour_rows.append(jnp.stack([own_slot, their_slot, mode_ids, lower_flag, occupied], axis=-1))
    return jnp.stack(colour_rows, axis=1).astype(jnp.int32)


def draw_match_edges(key, part):
    return match_tables(jax.random.fold_in(key, 11))


def left_tables(key):
    subkeys = jax.random.split(key, 8)
    blocks = jnp.arange(N_TIER, dtype=jnp.int32)
    orders = jax.vmap(lambda sub: jax.random.permutation(sub, 2 * REACH))(jax.random.split(subkeys[0], N_TIER))
    picked = orders[:, :LEFT_CAP].astype(jnp.int32)
    offsets = jnp.where(picked < REACH, picked - REACH, picked - REACH + 1)
    src_block = (blocks[:, None] + offsets) % N_TIER
    src_slot = jax.random.randint(subkeys[1], (N_TIER, LEFT_CAP), 0, MAT_DEV)
    target_slot = jax.random.randint(subkeys[2], (N_TIER, LEFT_CAP), 0, MAT_DEV)
    mode_ids = jax.random.randint(subkeys[3], (N_TIER, LEFT_CAP), 0, KMODES)
    lower_flag = jax.random.randint(subkeys[4], (N_TIER, LEFT_CAP), 0, 2)
    occupied = jax.random.randint(subkeys[5], (N_TIER, LEFT_CAP), 1, 4)
    rows = jnp.stack([target_slot, src_block * MAT_DEV + src_slot, mode_ids, lower_flag, occupied], axis=-1)
    counts = jax.random.randint(subkeys[6], (N_TIER,), 1, LEFT_CAP // 2 + 1)
    busiest = jax.random.randint(subkeys[7], (), 0, N_TIER)
    counts = jnp.where(blocks == busiest, LEFT_CAP, counts)
    return (rows.astype(jnp.int32), counts.astype(jnp.int32))


def draw_left_rows(key, part):
    return left_tables(jax.random.fold_in(key, 23))[0]


def draw_left_count(key, part):
    return left_tables(jax.random.fold_in(key, 23))[1]


def levels(key, shape, shards, least, top_value):
    level, own = 1.0, jax.random.fold_in(key, 6)
    for dim, parts in shards:
        draws = jnp.exp(jax.random.uniform(jax.random.fold_in(own, dim), (parts,), jnp.float32, least / len(shards), top_value / len(shards)))
        level = level * jnp.repeat(draws, shape[dim] // parts).reshape([-1 if axis == dim else 1 for axis in range(len(shape))])
    return level


def gaussian(key, extent, scale, limit, cuts=(), kind=jnp.bfloat16):
    factor_of = levels(key, extent, cuts, -0.22, 0.18) if cuts else 1.0
    drawn = jax.random.normal(key, extent, jnp.float32) * scale * factor_of
    return jnp.minimum(jnp.maximum(drawn, -limit), limit).astype(kind)


def setup_inputs(seed: int = 0, part: int = 0) -> dict:
    seeds = jax.random.split(jax.random.key(seed), 9)
    part_splits = jax.random.split(jax.random.fold_in(seeds[8], part), 9)
    rho = gaussian(part_splits[0], (MATRICES, 2, ORDER, ORDER), 1.0, 6.0, ((0, 16),), jnp.float32)
    hamiltonian = gaussian(seeds[1], (ORDER, ORDER), ORDER ** -0.5, 0.375, (), jnp.float32)
    couplings = gaussian(seeds[2], (KMODES, ORDER, ORDER), ORDER ** -0.5, 0.375, (), jnp.float32)
    bath_coef = jnp.clip(jax.random.uniform(part_splits[3], (KMODES, 2), jnp.float32, 0.3, 1.5), 0.3, 1.5)
    damping = jnp.clip(jnp.exp(math.log(3.0) - 2.7080502 * jax.random.uniform(part_splits[4], (MATRICES,), jnp.float32) ** levels(part_splits[4], (MATRICES,), ((0, 16),), -0.2, 0.2)), 0.2, 3.0)
    match_edges = draw_match_edges(jax.random.fold_in(seeds[8], 71), part)
    left_rows = draw_left_rows(jax.random.fold_in(seeds[8], 71), part)
    left_count = draw_left_count(jax.random.fold_in(seeds[8], 71), part)
    return dict(rho=rho, hamiltonian=hamiltonian, couplings=couplings, bath_coef=bath_coef, damping=damping, match_edges=match_edges, left_rows=left_rows, left_count=left_count)


step_size = 0.1

def commute_hamiltonian(density, hamiltonian):
    left_side = jnp.einsum('ab,nxbc->nxac', hamiltonian, density, precision=lax.Precision.HIGHEST)
    right_side = jnp.einsum('nxab,bc->nxac', density, hamiltonian, precision=lax.Precision.HIGHEST)
    difference = left_side - right_side
    return jnp.stack([difference[:, 1], -difference[:, 0]], axis=1)

def edge_terms(sources, mode_ids, lower_flags, occupied, couplings, bath_coef):
    chosen = jnp.take(couplings, mode_ids, axis=0)
    left_prod = jnp.einsum('rab,rxbc->rxac', chosen, sources, precision=lax.Precision.HIGHEST)
    right_prod = jnp.einsum('rxab,rbc->rxac', sources, chosen, precision=lax.Precision.HIGHEST)
    is_lower = lower_flags == 1
    real_coef = jnp.where(is_lower, jnp.ones_like(bath_coef[:, 0])[0], jnp.take(bath_coef[:, 0], mode_ids))
    imag_coef = jnp.where(is_lower, jnp.zeros_like(bath_coef[:, 1])[0], jnp.take(bath_coef[:, 1], mode_ids))
    root_occ = jnp.sqrt(occupied.astype(jnp.float32))
    difference = left_prod - right_prod
    summed = left_prod + right_prod
    real_part = real_coef[:, None, None] * difference[:, 0] - imag_coef[:, None, None] * summed[:, 1]
    imag_part = real_coef[:, None, None] * difference[:, 1] + imag_coef[:, None, None] * summed[:, 0]
    return root_occ[:, None, None, None] * jnp.stack([imag_part, -real_part], axis=1)

def reference(rho, hamiltonian, couplings, bath_coef, damping, match_edges, left_rows, left_count):
    blocks = jnp.arange(N_TIER, dtype=jnp.int32)
    targets, anchors, mode_ids, lower_flags, occupied, weights = ([], [], [], [], [], [])
    for colour in range(COLOURS):
        stride = 2 ** colour
        upper_half = blocks // stride % 2
        partner = blocks + stride - 2 * stride * upper_half
        edge_table = match_edges[:, colour]
        targets.append((blocks[:, None] * MAT_DEV + edge_table[:, :, 0]).reshape(-1))
        anchors.append((partner[:, None] * MAT_DEV + edge_table[:, :, 1]).reshape(-1))
        mode_ids.append(edge_table[:, :, 2].reshape(-1))
        lower_flags.append(edge_table[:, :, 3].reshape(-1))
        occupied.append(edge_table[:, :, 4].reshape(-1))
        weights.append(jnp.ones((N_TIER * PAIRS,), jnp.float32))
    live_rows = jnp.arange(LEFT_CAP, dtype=jnp.int32)[None, :] < left_count[:, None]
    targets.append((blocks[:, None] * MAT_DEV + left_rows[:, :, 0]).reshape(-1))
    anchors.append(left_rows[:, :, 1].reshape(-1))
    mode_ids.append(left_rows[:, :, 2].reshape(-1))
    lower_flags.append(left_rows[:, :, 3].reshape(-1))
    occupied.append(left_rows[:, :, 4].reshape(-1))
    weights.append(live_rows.reshape(-1).astype(jnp.float32))
    targets = jnp.concatenate(targets).astype(jnp.int32)
    anchors = jnp.concatenate(anchors).astype(jnp.int32)
    mode_ids = jnp.concatenate(mode_ids).astype(jnp.int32)
    lower_flags = jnp.concatenate(lower_flags)
    occupied = jnp.concatenate(occupied)
    weights = jnp.concatenate(weights)

    def derivative(density):
        sources = jnp.take(density, anchors, axis=0)
        row_terms = edge_terms(sources, mode_ids, lower_flags, occupied, couplings, bath_coef)
        row_terms = row_terms * weights[:, None, None, None]
        coupled = jax.ops.segment_sum(row_terms, targets, num_segments=MATRICES)
        return commute_hamiltonian(density, hamiltonian) - damping[:, None, None, None] * density + coupled
    first_slope = derivative(rho)
    middle = rho + step_size * first_slope
    second_slope = derivative(middle)
    return rho + 0.5 * step_size * (first_slope + second_slope)
```

```python
import functools

import jax
import jax.numpy as jnp
from jax import lax
from jax.experimental import pallas as pl
from jax.experimental.pallas import tpu as pltpu
from jax.sharding import PartitionSpec as P

REACH = 4
STEP = 0.1
F32 = jnp.float32
BF16 = jnp.bfloat16


def split(value):
    high = value.astype(BF16)
    low = (value - high.astype(F32)).astype(BF16)
    return high, low


def flip(index, stride):
    return index + stride - 2 * stride * ((index // stride) % 2)


def kernel(
    tier_size,
    colours,
    rho_ref,
    ham_ref,
    coup_ref,
    bath_ref,
    damp_ref,
    match_ref,
    left_ref,
    count_ref,
    out_ref,
    first_ref,
    term_ref,
    packed,
    arrived,
    op_left,
    op_right,
    send_sem,
    recv_sem,
):
    me = lax.axis_index("tier")
    mats = rho_ref.shape[0]
    order = rho_ref.shape[2]
    modes = coup_ref.shape[0]
    left_cap = left_ref.shape[1]
    deltas = [d for d in range(-REACH, 0)] + [d for d in range(1, REACH + 1)]
    rows = colours + len(deltas)

    targets = [flip(me, 2**c) for c in range(colours)]
    targets += [lax.rem(me - d + tier_size, tier_size) for d in deltas]

    barrier = pltpu.get_barrier_semaphore()
    for device in targets:
        pl.semaphore_signal(barrier, inc=1, device_id={"tier": device}, device_id_type=pl.DeviceIdType.MESH)
    pl.semaphore_wait(barrier, rows)

    def asked_slot(delta):
        asker = lax.rem(me - delta + tier_size, tier_size)
        slot = jnp.int32(0)
        for j in range(left_cap):
            source = left_ref[asker, j, 1]
            hit = (source // mats == me) & (j < count_ref[asker])
            slot = jnp.where(hit, source % mats, slot)
        return slot

    slots = [match_ref[c, 0] for c in range(colours)] + [asked_slot(d) for d in deltas]

    def copies(stage):
        return [
            pltpu.make_async_remote_copy(
                src_ref=packed.at[i],
                dst_ref=arrived.at[stage, i],
                send_sem=send_sem.at[stage, i],
                recv_sem=recv_sem.at[stage, i],
                device_id={"tier": targets[i]},
                device_id_type=pl.DeviceIdType.MESH,
            )
            for i in range(rows)
        ]

    def products(value, left, right):
        re_high, re_low = split(value[0])
        im_high, im_low = split(value[1])
        column = jnp.concatenate(
            [
                jnp.concatenate([re_high, re_low, re_high], axis=0),
                jnp.concatenate([im_high, im_low, im_high], axis=0),
            ],
            axis=1,
        )
        row = jnp.concatenate(
            [
                jnp.concatenate([re_high, re_low, re_high], axis=1),
                jnp.concatenate([im_high, im_low, im_high], axis=1),
            ],
            axis=0,
        )
        p = jnp.dot(left, column, preferred_element_type=F32)
        r = jnp.dot(row, right, preferred_element_type=F32)
        return p[:, :order], p[:, order:], r[:order], r[order:]

    def row_facts(i):
        c = jnp.minimum(i, colours - 1)
        is_match = i < colours
        q = i - colours
        delta = jnp.where(q < REACH, q - REACH, q - REACH + 1)
        source = lax.rem(me + delta + tier_size, tier_size)
        target, mode, flag, occ, weight = jnp.int32(0), jnp.int32(0), jnp.int32(0), jnp.int32(0), jnp.int32(0)
        for j in range(left_cap):
            hit = (left_ref[me, j, 1] // mats == source) & (j < count_ref[me])
            target = jnp.where(hit, left_ref[me, j, 0], target)
            mode = jnp.where(hit, left_ref[me, j, 2], mode)
            flag = jnp.where(hit, left_ref[me, j, 3], flag)
            occ = jnp.where(hit, left_ref[me, j, 4], occ)
            weight = jnp.where(hit, 1, weight)
        target = jnp.where(is_match, match_ref[c, 0], target)
        mode = jnp.where(is_match, match_ref[c, 2], mode)
        flag = jnp.where(is_match, match_ref[c, 3], flag)
        occ = jnp.where(is_match, match_ref[c, 4], occ)
        weight = jnp.where(is_match, 1, weight)
        a = jnp.where(flag == 1, F32(1.0), bath_ref[mode, 0])
        b = jnp.where(flag == 1, F32(0.0), bath_ref[mode, 1])
        return target, mode, a, b, occ, weight

    def handle_row(i, stage, scale, acc):
        pltpu.make_async_remote_copy(
            src_ref=packed.at[i],
            dst_ref=arrived.at[stage, i],
            send_sem=send_sem.at[stage, i],
            recv_sem=recv_sem.at[stage, i],
            device_id={"tier": targets[0]},
            device_id_type=pl.DeviceIdType.MESH,
        ).wait_recv()
        target, mode, a, b, occ, weight = row_facts(i)
        p_re, p_im, r_re, r_im = products(arrived[stage, i], op_left[mode], op_right[mode])
        root = jnp.sqrt(jnp.full((1, order), occ, jnp.int32).astype(F32)) * weight.astype(F32) * scale
        ca = root * a
        cb = root * b
        term_ref[0] = ca * (p_im - r_im) + cb * (p_re + r_re)
        term_ref[1] = cb * (p_im + r_im) - ca * (p_re - r_re)

        def add(s, carry):
            chosen = jnp.where(target == s, F32(1.0), F32(0.0))
            acc[s] = acc[s] + chosen * term_ref[...]
            return carry

        lax.fori_loop(0, mats, add, 0)

    def pack(source):
        for i in range(rows):
            packed[i] = source[slots[i]]

    pack(rho_ref)
    sends = copies(0)
    for copy in sends:
        copy.start()

    def prepare(k, carry):
        high, low = split(coup_ref[k])
        op_left[k] = jnp.concatenate([high, high, low], axis=1)
        op_right[k] = jnp.concatenate([high, high, low], axis=0)
        return carry

    lax.fori_loop(0, modes, prepare, 0)
    high, low = split(ham_ref[...])
    op_left[modes] = jnp.concatenate([high, high, low], axis=1)
    op_right[modes] = jnp.concatenate([high, high, low], axis=0)

    def own(n, carry):
        value = rho_ref[n]
        p_re, p_im, r_re, r_im = products(value, op_left[modes], op_right[modes])
        first_ref[n, 0] = (p_im - r_im) - damp_ref[n] * value[0]
        first_ref[n, 1] = (r_re - p_re) - damp_ref[n] * value[1]
        return carry

    lax.fori_loop(0, mats, own, 0)

    def row_first(i, carry):
        handle_row(i, 0, F32(1.0), first_ref)
        return carry

    lax.fori_loop(0, rows, row_first, 0)
    for copy in sends:
        copy.wait_send()

    pack(first_ref)
    sends = copies(1)
    for copy in sends:
        copy.start()

    half = F32(0.5 * STEP * STEP)

    def own_second(n, carry):
        value = first_ref[n]
        p_re, p_im, r_re, r_im = products(value, op_left[modes], op_right[modes])
        out_ref[n, 0] = rho_ref[n, 0] + F32(STEP) * value[0] + half * ((p_im - r_im) - damp_ref[n] * value[0])
        out_ref[n, 1] = rho_ref[n, 1] + F32(STEP) * value[1] + half * ((r_re - p_re) - damp_ref[n] * value[1])
        return carry

    lax.fori_loop(0, mats, own_second, 0)

    def row_second(i, carry):
        handle_row(i, 1, half, out_ref)
        return carry

    lax.fori_loop(0, rows, row_second, 0)
    for copy in sends:
        copy.wait_send()


def body(tier_size, rho, hamiltonian, couplings, bath_coef, damping, match_edges, left_rows, left_count):
    mats, _, order, _ = rho.shape
    modes = couplings.shape[0]
    table = match_edges.reshape(-1, match_edges.shape[-1])
    colours = table.shape[0]
    rows = colours + 2 * REACH
    vmem = pl.BlockSpec(memory_space=pltpu.VMEM)
    smem = pl.BlockSpec(memory_space=pltpu.SMEM)
    return pl.pallas_call(
        functools.partial(kernel, tier_size, colours),
        out_shape=jax.ShapeDtypeStruct(rho.shape, F32),
        in_specs=[vmem, vmem, vmem, smem, smem, smem, smem, smem],
        out_specs=vmem,
        scratch_shapes=[
            pltpu.VMEM(rho.shape, F32),
            pltpu.VMEM((2, order, order), F32),
            pltpu.VMEM((rows, 2, order, order), F32),
            pltpu.VMEM((2, rows, 2, order, order), F32),
            pltpu.VMEM((modes + 1, order, 3 * order), BF16),
            pltpu.VMEM((modes + 1, 3 * order, order), BF16),
            pltpu.SemaphoreType.DMA((2, rows)),
            pltpu.SemaphoreType.DMA((2, rows)),
        ],
        compiler_params=pltpu.CompilerParams(
            collective_id=0, has_side_effects=True, vmem_limit_bytes=60 * 1024 * 1024
        ),
    )(rho, hamiltonian, couplings, bath_coef, damping, table, left_rows, left_count)


def solution(mesh):
    placed = (
        P(("groups", "tier"), None, None, None),
        P(),
        P(),
        P("groups", None),
        P(("groups", "tier")),
        P("tier", None, None, None),
        P(),
        P(),
    )
    return jax.shard_map(
        functools.partial(body, mesh.shape["tier"]),
        mesh=mesh,
        in_specs=placed,
        out_specs=P(("groups", "tier"), None, None, None),
        check_vma=False,
    )
```

```python
import functools

import jax
import jax.numpy as jnp
from jax import lax
from jax.experimental import pallas as pl
from jax.experimental.pallas import tpu as pltpu
from jax.sharding import PartitionSpec as P

REACH = 4
STEP = 0.1
F32 = jnp.float32
BF16 = jnp.bfloat16


def split(value):
    high = value.astype(BF16)
    low = (value - high.astype(F32)).astype(BF16)
    return high, low


def flip(index, stride):
    return index + stride - 2 * stride * ((index // stride) % 2)


def kernel(
    tier_size,
    colours,
    rho_any,
    ham_ref,
    coup_ref,
    bath_ref,
    damp_ref,
    match_ref,
    left_ref,
    count_ref,
    out_ref,
    rho_ref,
    rho_sem,
    first_ref,
    term_ref,
    packed,
    arrived,
    op_left,
    op_right,
    send_sem,
    recv_sem,
):
    load = pltpu.make_async_copy(rho_any, rho_ref, rho_sem)
    load.start()
    me = lax.axis_index("tier")
    mats = rho_ref.shape[0]
    order = rho_ref.shape[2]
    modes = coup_ref.shape[0]
    left_cap = left_ref.shape[1]
    deltas = [d for d in range(-REACH, 0)] + [d for d in range(1, REACH + 1)]
    rows = colours + len(deltas)

    targets = [flip(me, 2**c) for c in range(colours)]
    targets += [lax.rem(me - d + tier_size, tier_size) for d in deltas]

    barrier = pltpu.get_barrier_semaphore()
    for device in targets:
        pl.semaphore_signal(barrier, inc=1, device_id={"tier": device}, device_id_type=pl.DeviceIdType.MESH)
    pl.semaphore_wait(barrier, rows)

    def asked_slot(delta):
        asker = lax.rem(me - delta + tier_size, tier_size)
        slot = jnp.int32(0)
        for j in range(left_cap):
            source = left_ref[1, j, asker]
            hit = (source // mats == me) & (j < count_ref[asker])
            slot = jnp.where(hit, source % mats, slot)
        return slot

    slots = [match_ref[c, 0] for c in range(colours)] + [asked_slot(d) for d in deltas]

    def copies(stage):
        return [
            pltpu.make_async_remote_copy(
                src_ref=packed.at[i],
                dst_ref=arrived.at[stage, i],
                send_sem=send_sem.at[stage, i],
                recv_sem=recv_sem.at[stage, i],
                device_id={"tier": targets[i]},
                device_id_type=pl.DeviceIdType.MESH,
            )
            for i in range(rows)
        ]

    def products(value, left, right):
        re_high, re_low = split(value[0])
        im_high, im_low = split(value[1])
        column = jnp.concatenate(
            [
                jnp.concatenate([re_high, re_low, re_high], axis=0),
                jnp.concatenate([im_high, im_low, im_high], axis=0),
            ],
            axis=1,
        )
        row = jnp.concatenate(
            [
                jnp.concatenate([re_high, re_low, re_high], axis=1),
                jnp.concatenate([im_high, im_low, im_high], axis=1),
            ],
            axis=0,
        )
        p = jnp.dot(left, column, preferred_element_type=F32)
        r = jnp.dot(row, right, preferred_element_type=F32)
        return p[:, :order], p[:, order:], r[:order], r[order:]

    def row_facts(i):
        c = jnp.minimum(i, colours - 1)
        is_match = i < colours
        q = i - colours
        delta = jnp.where(q < REACH, q - REACH, q - REACH + 1)
        source = lax.rem(me + delta + tier_size, tier_size)
        target, mode, flag, occ, weight = jnp.int32(0), jnp.int32(0), jnp.int32(0), jnp.int32(0), jnp.int32(0)
        for j in range(left_cap):
            hit = (left_ref[1, j, me] // mats == source) & (j < count_ref[me])
            target = jnp.where(hit, left_ref[0, j, me], target)
            mode = jnp.where(hit, left_ref[2, j, me], mode)
            flag = jnp.where(hit, left_ref[3, j, me], flag)
            occ = jnp.where(hit, left_ref[4, j, me], occ)
            weight = jnp.where(hit, 1, weight)
        target = jnp.where(is_match, match_ref[c, 0], target)
        mode = jnp.where(is_match, match_ref[c, 2], mode)
        flag = jnp.where(is_match, match_ref[c, 3], flag)
        occ = jnp.where(is_match, match_ref[c, 4], occ)
        weight = jnp.where(is_match, 1, weight)
        a = jnp.where(flag == 1, F32(1.0), bath_ref[0, mode])
        b = jnp.where(flag == 1, F32(0.0), bath_ref[1, mode])
        return target, mode, a, b, occ, weight

    def handle_row(i, stage, scale, acc):
        pltpu.make_async_remote_copy(
            src_ref=packed.at[i],
            dst_ref=arrived.at[stage, i],
            send_sem=send_sem.at[stage, i],
            recv_sem=recv_sem.at[stage, i],
            device_id={"tier": targets[0]},
            device_id_type=pl.DeviceIdType.MESH,
        ).wait_recv()
        target, mode, a, b, occ, weight = row_facts(i)
        p_re, p_im, r_re, r_im = products(arrived[stage, i], op_left[mode], op_right[mode])
        root = jnp.sqrt(jnp.full((1, order), occ, jnp.int32).astype(F32)) * weight.astype(F32) * scale
        ca = root * a
        cb = root * b
        term_ref[0] = ca * (p_im - r_im) + cb * (p_re + r_re)
        term_ref[1] = cb * (p_im + r_im) - ca * (p_re - r_re)

        def add(s, carry):
            chosen = jnp.where(target == s, F32(1.0), F32(0.0))
            acc[s] = acc[s] + chosen * term_ref[...]
            return carry

        lax.fori_loop(0, mats, add, 0)

    def pack_and_send(source, stage):
        sends = copies(stage)
        for i in range(rows):
            packed[i] = source[slots[i]]
            if i > 0:
                sends[i - 1].start()
        sends[rows - 1].start()
        return sends

    load.wait()
    sends = pack_and_send(rho_ref, 0)

    def prepare(k, carry):
        high, low = split(coup_ref[k])
        op_left[k] = jnp.concatenate([high, high, low], axis=1)
        op_right[k] = jnp.concatenate([high, high, low], axis=0)
        return carry

    lax.fori_loop(0, modes, prepare, 0)
    high, low = split(ham_ref[...])
    op_left[modes] = jnp.concatenate([high, high, low], axis=1)
    op_right[modes] = jnp.concatenate([high, high, low], axis=0)

    def own(n, carry):
        value = rho_ref[n]
        p_re, p_im, r_re, r_im = products(value, op_left[modes], op_right[modes])
        first_ref[n, 0] = (p_im - r_im) - damp_ref[n] * value[0]
        first_ref[n, 1] = (r_re - p_re) - damp_ref[n] * value[1]
        return carry

    lax.fori_loop(0, mats, own, 0)

    def row_first(i, carry):
        handle_row(i, 0, F32(1.0), first_ref)
        return carry

    lax.fori_loop(0, rows, row_first, 0)
    for copy in sends:
        copy.wait_send()

    sends = pack_and_send(first_ref, 1)

    half = F32(0.5 * STEP * STEP)

    def own_second(n, carry):
        value = first_ref[n]
        p_re, p_im, r_re, r_im = products(value, op_left[modes], op_right[modes])
        out_ref[n, 0] = rho_ref[n, 0] + F32(STEP) * value[0] + half * ((p_im - r_im) - damp_ref[n] * value[0])
        out_ref[n, 1] = rho_ref[n, 1] + F32(STEP) * value[1] + half * ((r_re - p_re) - damp_ref[n] * value[1])
        return carry

    lax.fori_loop(0, mats, own_second, 0)

    def row_second(i, carry):
        handle_row(i, 1, half, out_ref)
        return carry

    lax.fori_loop(0, rows, row_second, 0)
    for copy in sends:
        copy.wait_send()


def body(tier_size, rho, hamiltonian, couplings, bath_coef, damping, match_edges, left_rows, left_count):
    mats, _, order, _ = rho.shape
    modes = couplings.shape[0]
    table = match_edges.reshape(-1, match_edges.shape[-1])
    colours = table.shape[0]
    rows = colours + 2 * REACH
    vmem = pl.BlockSpec(memory_space=pltpu.VMEM)
    smem = pl.BlockSpec(memory_space=pltpu.SMEM)
    return pl.pallas_call(
        functools.partial(kernel, tier_size, colours),
        out_shape=pltpu.VMEM(rho.shape, F32),
        in_specs=[pl.BlockSpec(memory_space=pl.ANY), vmem, vmem, smem, smem, smem, smem, smem],
        out_specs=vmem,
        scratch_shapes=[
            pltpu.VMEM(rho.shape, F32),
            pltpu.SemaphoreType.DMA,
            pltpu.VMEM(rho.shape, F32),
            pltpu.VMEM((2, order, order), F32),
            pltpu.VMEM((rows, 2, order, order), F32),
            pltpu.VMEM((2, rows, 2, order, order), F32),
            pltpu.VMEM((modes + 1, order, 3 * order), BF16),
            pltpu.VMEM((modes + 1, 3 * order, order), BF16),
            pltpu.SemaphoreType.DMA((2, rows)),
            pltpu.SemaphoreType.DMA((2, rows)),
        ],
        compiler_params=pltpu.CompilerParams(
            collective_id=0, has_side_effects=True, vmem_limit_bytes=50 * 1024 * 1024
        ),
    )(rho, hamiltonian, couplings, bath_coef.T, damping, table, left_rows.transpose(2, 1, 0), left_count)


def solution(mesh):
    placed = (
        P(("groups", "tier"), None, None, None),
        P(),
        P(),
        P("groups", None),
        P(("groups", "tier")),
        P("tier", None, None, None),
        P(),
        P(),
    )
    return jax.shard_map(
        functools.partial(body, mesh.shape["tier"]),
        mesh=mesh,
        in_specs=placed,
        out_specs=P(("groups", "tier"), None, None, None),
        check_vma=False,
    )
```

```python
import functools

import jax
import jax.numpy as jnp
from jax import lax
from jax.experimental import pallas as pl
from jax.experimental.pallas import tpu as pltpu
from jax.sharding import PartitionSpec as P

REACH = 4
STEP = 0.1
F32 = jnp.float32
BF16 = jnp.bfloat16


def split(value):
    high = value.astype(BF16)
    low = (value - high.astype(F32)).astype(BF16)
    return high, low


def flip(index, stride):
    return index + stride - 2 * stride * ((index // stride) % 2)


def kernel(
    tier_size,
    colours,
    rho_any,
    ham_any,
    coup_any,
    bath_ref,
    damp_ref,
    match_ref,
    left_ref,
    count_ref,
    out_ref,
    rho_ref,
    ham_ref,
    coup_ref,
    load_sem,
    first_ref,
    term_ref,
    packed,
    arrived,
    op_left,
    op_right,
    send_sem,
    recv_sem,
):
    loads = [
        pltpu.make_async_copy(rho_any, rho_ref, load_sem.at[0]),
        pltpu.make_async_copy(ham_any, ham_ref, load_sem.at[1]),
        pltpu.make_async_copy(coup_any, coup_ref, load_sem.at[2]),
    ]
    for load in loads:
        load.start()
    me = lax.axis_index("tier")
    mats = rho_ref.shape[0]
    order = rho_ref.shape[2]
    modes = coup_ref.shape[0]
    left_cap = left_ref.shape[1]
    deltas = [d for d in range(REACH, 0, -1)] + [d for d in range(-1, -REACH - 1, -1)]
    rows = colours + len(deltas)

    targets = [flip(me, 2**c) for c in range(colours)]
    targets += [lax.rem(me - d + tier_size, tier_size) for d in deltas]

    barrier = pltpu.get_barrier_semaphore()
    for device in targets:
        pl.semaphore_signal(barrier, inc=1, device_id={"tier": device}, device_id_type=pl.DeviceIdType.MESH)
    pl.semaphore_wait(barrier, rows)

    def asked_slot(delta):
        asker = lax.rem(me - delta + tier_size, tier_size)
        slot = jnp.int32(0)
        for j in range(left_cap):
            source = left_ref[1, j, asker]
            hit = (source // mats == me) & (j < count_ref[asker])
            slot = jnp.where(hit, source % mats, slot)
        return slot

    slots = [match_ref[c, 0] for c in range(colours)] + [asked_slot(d) for d in deltas]

    def copies(stage):
        return [
            pltpu.make_async_remote_copy(
                src_ref=packed.at[i],
                dst_ref=arrived.at[stage, i],
                send_sem=send_sem.at[stage, i],
                recv_sem=recv_sem.at[stage, i],
                device_id={"tier": targets[i]},
                device_id_type=pl.DeviceIdType.MESH,
            )
            for i in range(rows)
        ]

    def products(value, left, right):
        re_high, re_low = split(value[0])
        im_high, im_low = split(value[1])
        column = jnp.concatenate(
            [
                jnp.concatenate([re_high, re_low, re_high], axis=0),
                jnp.concatenate([im_high, im_low, im_high], axis=0),
            ],
            axis=1,
        )
        row = jnp.concatenate(
            [
                jnp.concatenate([re_high, re_low, re_high], axis=1),
                jnp.concatenate([im_high, im_low, im_high], axis=1),
            ],
            axis=0,
        )
        p = jnp.dot(left, column, preferred_element_type=F32)
        r = jnp.dot(row, right, preferred_element_type=F32)
        return p[:, :order], p[:, order:], r[:order], r[order:]

    def row_facts(i):
        c = jnp.minimum(i, colours - 1)
        is_match = i < colours
        q = i - colours
        delta = jnp.where(q < REACH, REACH - q, REACH - 1 - q)
        source = lax.rem(me + delta + tier_size, tier_size)
        target, mode, flag, occ, weight = jnp.int32(0), jnp.int32(0), jnp.int32(0), jnp.int32(0), jnp.int32(0)
        for j in range(left_cap):
            hit = (left_ref[1, j, me] // mats == source) & (j < count_ref[me])
            target = jnp.where(hit, left_ref[0, j, me], target)
            mode = jnp.where(hit, left_ref[2, j, me], mode)
            flag = jnp.where(hit, left_ref[3, j, me], flag)
            occ = jnp.where(hit, left_ref[4, j, me], occ)
            weight = jnp.where(hit, 1, weight)
        target = jnp.where(is_match, match_ref[c, 0], target)
        mode = jnp.where(is_match, match_ref[c, 2], mode)
        flag = jnp.where(is_match, match_ref[c, 3], flag)
        occ = jnp.where(is_match, match_ref[c, 4], occ)
        weight = jnp.where(is_match, 1, weight)
        a = jnp.where(flag == 1, F32(1.0), bath_ref[0, mode])
        b = jnp.where(flag == 1, F32(0.0), bath_ref[1, mode])
        return target, mode, a, b, occ, weight

    def handle_row(i, stage, scale, acc):
        pltpu.make_async_remote_copy(
            src_ref=packed.at[i],
            dst_ref=arrived.at[stage, i],
            send_sem=send_sem.at[stage, i],
            recv_sem=recv_sem.at[stage, i],
            device_id={"tier": targets[0]},
            device_id_type=pl.DeviceIdType.MESH,
        ).wait_recv()
        target, mode, a, b, occ, weight = row_facts(i)
        p_re, p_im, r_re, r_im = products(arrived[stage, i], op_left[mode], op_right[mode])
        root = jnp.sqrt(jnp.full((1, order), occ, jnp.int32).astype(F32)) * weight.astype(F32) * scale
        ca = root * a
        cb = root * b
        term_ref[0] = ca * (p_im - r_im) + cb * (p_re + r_re)
        term_ref[1] = cb * (p_im + r_im) - ca * (p_re - r_re)

        def add(s, carry):
            chosen = jnp.where(target == s, F32(1.0), F32(0.0))
            acc[s] = acc[s] + chosen * term_ref[...]
            return carry

        lax.fori_loop(0, mats, add, 0)

    def pack_and_send(source, stage):
        sends = copies(stage)
        for i in range(rows):
            packed[i] = source[slots[i]]
            if i > 0:
                sends[i - 1].start()
        sends[rows - 1].start()
        return sends

    loads[0].wait()
    sends = pack_and_send(rho_ref, 0)
    loads[1].wait()
    loads[2].wait()

    def prepare(k, carry):
        high, low = split(coup_ref[k])
        op_left[k] = jnp.concatenate([high, high, low], axis=1)
        op_right[k] = jnp.concatenate([high, high, low], axis=0)
        return carry

    lax.fori_loop(0, modes, prepare, 0)
    high, low = split(ham_ref[...])
    op_left[modes] = jnp.concatenate([high, high, low], axis=1)
    op_right[modes] = jnp.concatenate([high, high, low], axis=0)

    def own(n, carry):
        value = rho_ref[n]
        p_re, p_im, r_re, r_im = products(value, op_left[modes], op_right[modes])
        first_ref[n, 0] = (p_im - r_im) - damp_ref[n] * value[0]
        first_ref[n, 1] = (r_re - p_re) - damp_ref[n] * value[1]
        return carry

    lax.fori_loop(0, mats, own, 0)

    def row_first(i, carry):
        handle_row(i, 0, F32(1.0), first_ref)
        return carry

    lax.fori_loop(0, rows, row_first, 0)
    for copy in sends:
        copy.wait_send()

    sends = pack_and_send(first_ref, 1)

    half = F32(0.5 * STEP * STEP)

    def own_second(n, carry):
        value = first_ref[n]
        p_re, p_im, r_re, r_im = products(value, op_left[modes], op_right[modes])
        out_ref[n, 0] = rho_ref[n, 0] + F32(STEP) * value[0] + half * ((p_im - r_im) - damp_ref[n] * value[0])
        out_ref[n, 1] = rho_ref[n, 1] + F32(STEP) * value[1] + half * ((r_re - p_re) - damp_ref[n] * value[1])
        return carry

    lax.fori_loop(0, mats, own_second, 0)

    def row_second(i, carry):
        handle_row(i, 1, half, out_ref)
        return carry

    lax.fori_loop(0, rows, row_second, 0)
    for copy in sends:
        copy.wait_send()


def body(tier_size, rho, hamiltonian, couplings, bath_coef, damping, match_edges, left_rows, left_count):
    mats, _, order, _ = rho.shape
    modes = couplings.shape[0]
    table = match_edges.reshape(-1, match_edges.shape[-1])
    colours = table.shape[0]
    rows = colours + 2 * REACH
    vmem = pl.BlockSpec(memory_space=pltpu.VMEM)
    hbm = pl.BlockSpec(memory_space=pl.ANY)
    smem = pl.BlockSpec(memory_space=pltpu.SMEM)
    return pl.pallas_call(
        functools.partial(kernel, tier_size, colours),
        out_shape=pltpu.VMEM(rho.shape, F32),
        in_specs=[hbm, hbm, hbm, smem, smem, smem, smem, smem],
        out_specs=vmem,
        scratch_shapes=[
            pltpu.VMEM(rho.shape, F32),
            pltpu.VMEM(hamiltonian.shape, F32),
            pltpu.VMEM(couplings.shape, F32),
            pltpu.SemaphoreType.DMA((3,)),
            pltpu.VMEM(rho.shape, F32),
            pltpu.VMEM((2, order, order), F32),
            pltpu.VMEM((rows, 2, order, order), F32),
            pltpu.VMEM((2, rows, 2, order, order), F32),
            pltpu.VMEM((modes + 1, order, 3 * order), BF16),
            pltpu.VMEM((modes + 1, 3 * order, order), BF16),
            pltpu.SemaphoreType.DMA((2, rows)),
            pltpu.SemaphoreType.DMA((2, rows)),
        ],
        compiler_params=pltpu.CompilerParams(
            collective_id=0, has_side_effects=True, vmem_limit_bytes=50 * 1024 * 1024
        ),
    )(rho, hamiltonian, couplings, bath_coef.T, damping, table, left_rows.transpose(2, 1, 0), left_count)


def solution(mesh):
    placed = (
        P(("groups", "tier"), None, None, None),
        P(),
        P(),
        P("groups", None),
        P(("groups", "tier")),
        P("tier", None, None, None),
        P(),
        P(),
    )
    return jax.shard_map(
        functools.partial(body, mesh.shape["tier"]),
        mesh=mesh,
        in_specs=placed,
        out_specs=P(("groups", "tier"), None, None, None),
        check_vma=False,
    )
```
